128 devices in a mesh: occ: 8 (over x, core), vir: 16 (over y, z).
Axes of the slice: x: 4, y: 4, z: 4, core: 2. Of those that a mesh axis runs over, the one named last changes fastest.
Arguments:
- amplitudes: bfloat16 [8, 2, 4096, 4096], P('occ', None, None, 'vir'), may hold values from -6 to 6
- coulomb: bfloat16 [8, 2, 4096, 4096], P('occ', None, None, 'vir'), may hold values from -6 to 6
- ladder_tiles: bfloat16 [256, 128, 128], P('vir'), may hold values from -0.1875 to 0.1875
- cycle_tiles: bfloat16 [256, 128, 128], P('vir'), may hold values from -0.25 to 0.25
- ladder_screen: int32 [32, 8], replicated, may hold values from 0 to 31, as said below
- tile_slot: int32 [256], replicated, may hold values from 0 to 255, each once
- cycle_screen: int32 [64, 4], replicated, may hold values from 0 to 63, as said below
- cycle_rows: int32 [32, 48], replicated, may hold values from 0 to 63, as said below
- cycle_count: int32 [32], replicated, may hold values from 1 to 48, 1024 in all
- slab_occ: int32 [8], replicated, may hold values from 0 to 399
- window_occ: int32 [2], replicated, may hold values from 0 to 399
- occ_energy: float32 [400], replicated, may hold values from -3 to -0.5
- vir_energy: float32 [4096], replicated, may hold values from 0.4 to 4
Outputs:
- updated: bfloat16 [8, 2, 4096, 4096], P('occ', None, None, 'vir')
The draws below stay inside these ranges and needn't reach their ends.
Inputs may be any that keep to these rules, and one draw needn't show every extreme that they name: `ladder_screen`: each row names 8 different tiles. `cycle_screen`: each row names 4 different row tiles. `cycle_rows`: each row names 48 different block columns; the first cycle_count of them are used. `cycle_count`: the counts sum to exactly 1024, and the largest is exactly 48.
All inputs are finite; a program needn't handle non-finite values.
Results may differ from the reference program's by a relative error of at most 0.003.
Values may be sent and summed in bfloat16 or wider, within the bound.
No kernel may reach another device: no remote copies, remote signals or barrier semaphores. Data moves between devices by JAX's collectives and lax.ppermute only.
A program may use at most 192 MiB of HBM per device.

```python
import math
import jax
import jax.numpy as jnp
import numpy as np
from jax import lax

VIRT = 4096
TILE = 128
NOCC = 400
OJ = 2
KL = 8
KZ = 4
RMOST = 48
RTOTAL = 1024
NVT = 32
OI = 8


def distinct_rows(key, count, span, keep):
    keys = jax.random.split(key, count)
    return jax.vmap(lambda single: jax.random.permutation(single, span)[:keep])(keys).astype(jnp.int32)


def draw_ladder_screen(key, part):
    return distinct_rows(jax.random.fold_in(key, 11), NVT, NVT, KL)


def draw_cycle_screen(key, part):
    return distinct_rows(jax.random.fold_in(key, 23), OJ * NVT, OJ * NVT, KZ)


def draw_cycle_rows(key, part):
    return distinct_rows(jax.random.fold_in(key, 37), NVT, OJ * NVT, RMOST)


def set_ends(drawn, key, smallest, largest):
    spot = [jax.random.randint(jax.random.fold_in(key, axis), (), 0, length) for axis, length in enumerate(drawn.shape)]
    longest = drawn.shape.index(max(drawn.shape))
    beside = spot[:longest] + [(spot[longest] + 1) % drawn.shape[longest]] + spot[longest + 1:]
    return drawn.at[tuple(spot)].set(smallest).at[tuple(beside)].set(largest)


def levels(rng, dims, cuts, smallest, top_value):
    level, own = 1.0, jax.random.fold_in(rng, 6)
    for dim, parts in cuts:
        steps = jnp.exp(jax.random.uniform(jax.random.fold_in(own, dim), (parts,), jnp.float32, smallest / len(cuts), top_value / len(cuts)))
        level = level * jnp.repeat(steps, dims[dim] // parts).reshape([-1 if axis == dim else 1 for axis in range(len(dims))])
    return level


def length_profile(count, total, bound, lean):
    portions = [(1 << 20) // math.isqrt(grade ** lean) + 1 for grade in range(2, count + 1)]
    spare, given = total - bound - (count - 1), [1] * (count - 1)
    while spare > 0:
        movable = [i for i in range(count - 1) if given[i] < bound]
        mass, budget = sum([portions[i] for i in movable]), spare
        for i in movable:
            more = min(bound - given[i], max(1, budget * portions[i] // mass), spare)
            given[i] = given[i] + more
            spare = spare - more
    return np.array([bound] + given)


def ragged_sizes(rng, count, total, most, skew):
    if count == 2:
        one = jax.random.randint(rng, (), max(1, total - most), min(most, total - 1) + 1)
        return jnp.stack([one, total - one])
    sizes = jnp.asarray(length_profile(count, total, most, skew), jnp.int32)
    twos = (count - 1) // 2
    giver, receiver = sizes[1:1 + 2 * twos:2], sizes[2:2 + 2 * twos:2]
    slack = jnp.minimum(giver - 1, most - receiver)
    passed = jax.random.randint(jax.random.fold_in(rng, 1), (twos,), 0, 1 << 20) % (slack + 1)
    sizes = sizes.at[1:1 + 2 * twos:2].set(giver - passed).at[2:2 + 2 * twos:2].set(receiver + passed)
    return sizes[jax.random.permutation(jax.random.fold_in(rng, 2), count)]


def centred(key, extent, deviation, most, cuts=(), held_as=jnp.bfloat16):
    array = jax.random.normal(key, extent, jnp.float32) * deviation
    if len(cuts) > 0:
        array = levels(key, extent, cuts, -0.22, 0.18) * array
    return jnp.clip(array, min=-most, max=most).astype(held_as)


def setup_inputs(seed: int = 0) -> dict:
    seeds = jax.random.split(jax.random.key(seed), 14)
    return {
        "amplitudes": centred(seeds[0], (OI, OJ, VIRT, VIRT), 1.0, 6.0, ((0, 8), (3, 16))),
        "coulomb": centred(seeds[1], (OI, OJ, VIRT, VIRT), 1.0, 6.0, ((0, 8), (3, 16))),
        "ladder_tiles": centred(seeds[2], (NVT * KL, TILE, TILE), (TILE * KL) ** -0.5, 0.1875, ((0, 16),)),
        "cycle_tiles": centred(seeds[3], (OJ * NVT * KZ, TILE, TILE), (TILE * KZ) ** -0.5, 0.25, ((0, 16),)),
        "ladder_screen": draw_ladder_screen(jax.random.fold_in(seeds[13], 71), 0),
        "tile_slot": jax.random.permutation(seeds[5], NVT * KL).astype(jnp.int32),
        "cycle_screen": draw_cycle_screen(jax.random.fold_in(seeds[13], 71), 0),
        "cycle_rows": draw_cycle_rows(jax.random.fold_in(seeds[13], 71), 0),
        "cycle_count": ragged_sizes(seeds[8], NVT, RTOTAL, RMOST, 2).astype(jnp.int32),
        "slab_occ": set_ends(jax.random.randint(seeds[9], (OI,), 0, NOCC), jax.random.fold_in(seeds[9], 1), 0, NOCC - 1).astype(jnp.int32),
        "window_occ": jax.random.randint(seeds[10], (OJ,), 0, NOCC).astype(jnp.int32),
        "occ_energy": jnp.clip(jax.random.uniform(seeds[11], (NOCC,), jnp.float32, -3.0, -0.5), -3.0, -0.5),
        "vir_energy": jnp.clip(jnp.exp(jax.random.uniform(seeds[12], (VIRT,), jnp.float32, math.log(0.4), math.log(4.0))), 0.4, 4.0),
    }


def reference(amplitudes, coulomb, ladder_tiles, cycle_tiles, ladder_screen, tile_slot, cycle_screen, cycle_rows, cycle_count, slab_occ, window_occ, occ_energy, vir_energy):
    chosen = ladder_tiles[tile_slot.reshape(NVT, KL)]
    cycle_sel = cycle_tiles.reshape(OJ * NVT, KZ, TILE, TILE)
    ends = jnp.cumsum(cycle_count).astype(jnp.int32)
    entry = jnp.arange(RTOTAL, dtype=jnp.int32)
    owner = jnp.sum((ends[None, :] <= entry[:, None]).astype(jnp.int32), axis=1).astype(jnp.int32)
    place = (entry - ends[owner] + cycle_count[owner]).astype(jnp.int32)
    columns = cycle_rows[owner, place]
    energy_j = occ_energy[window_occ]

    def one_row(index):
        amp = lax.dynamic_index_in_dim(amplitudes, index, 0, keepdims=False)
        near = lax.dynamic_index_in_dim(coulomb, index, 0, keepdims=False)
        arranged = amp.transpose(1, 0, 2).reshape(NVT, TILE, OJ * VIRT)
        total = jnp.zeros((NVT, TILE, OJ * VIRT), jnp.float32)
        for level in range(KL):
            total = total + jnp.einsum('arc,ace->are', chosen[:, level].astype(jnp.float32), arranged[ladder_screen[:, level]].astype(jnp.float32))
        ladder = total.reshape(VIRT, OJ, VIRT).transpose(1, 0, 2)
        tiles = amp.reshape(OJ, NVT, TILE, NVT, TILE).transpose(0, 3, 1, 2, 4).reshape(OJ * NVT, NVT, TILE, TILE)
        part = jnp.zeros((RTOTAL, TILE, TILE), jnp.float32)
        for level in range(KZ):
            picked = tiles[cycle_screen[columns, level], owner]
            part = part + jnp.einsum('erc,ecb->erb', picked.astype(jnp.float32), cycle_sel[columns, level].astype(jnp.float32))
        cycle = jnp.zeros((OJ * NVT, NVT, TILE, TILE), jnp.float32).at[columns, owner].add(part).astype(jnp.bfloat16)
        cycle = cycle.reshape(OJ, NVT, NVT, TILE, TILE).transpose(0, 2, 3, 1, 4).reshape(OJ, VIRT, VIRT)
        energy_i = occ_energy[slab_occ[index]]
        denominator = vir_energy[None, :, None] + vir_energy[None, None, :] - energy_i - energy_j[:, None, None]
        value = near.astype(jnp.float32) + ladder + cycle.astype(jnp.float32)
        return (value / denominator).astype(jnp.bfloat16)

    return lax.map(one_row, jnp.arange(OI, dtype=jnp.int32))
```

```python
import jax
import jax.numpy as jnp
from jax import lax
from jax.experimental import pallas as pl
from jax.experimental.pallas import tpu as pltpu
from jax.sharding import PartitionSpec as P

F32 = jnp.float32
BF16 = jnp.bfloat16


def tile_of(ref, slot):
    per_dev = ref.shape[0] * ref.shape[2]
    return ref[(slot % per_dev) // ref.shape[2], slot // per_dev, slot % ref.shape[2]]


def cycle_kernel(screen, rows, count, place, t_ref, z_ref, out_ref, mask):
    step = pl.program_id(0)
    tile = z_ref.shape[-1]
    height, width = t_ref.shape[2:]
    tiles_here, tiles_wide = height // tile, width // tile
    window, keep = t_ref.shape[1], screen.shape[1]
    tile_count = screen.shape[0] // window
    first = place[1] * tiles_here

    @pl.when(step == 0)
    def _():
        for a in range(tiles_here):

            @pl.loop(0, mask.shape[1])
            def _(q):
                mask[a, q] = 0

            @pl.loop(0, count[first + a])
            def _(e):
                mask[a, rows[first + a, e]] = 1

    for j in range(window):
        for b in range(tiles_wide):
            q = j * tile_count + step * tiles_wide + b
            left, right = [], []
            for m in range(keep):
                u = screen[q, m]
                c = u % tile_count
                lane = pl.multiple_of((c % tiles_wide) * tile, tile)
                left.append(t_ref[c // tiles_wide, u // tile_count, :, pl.ds(lane, tile)])
                right.append(tile_of(z_ref, q * keep + m))
            part = jnp.dot(
                jnp.concatenate(left, axis=1),
                jnp.concatenate(right, axis=0),
                preferred_element_type=F32,
            )
            for a in range(tiles_here):
                rows_a = part[a * tile : (a + 1) * tile]
                used = jnp.full(rows_a.shape, mask[a, q], jnp.int32) > 0
                out_ref[0, j, a * tile : (a + 1) * tile, b * tile : (b + 1) * tile] = jnp.where(
                    used, rows_a, 0.0
                ).astype(BF16)


def ladder_kernel(screen, slots, t_ref, w_ref, near_ref, out_ref):
    step = pl.program_id(0)
    tile = w_ref.shape[-1]
    keep = screen.shape[1]
    group = out_ref.shape[1] // tile
    for a in range(group):
        block = step * group + a
        left = jnp.concatenate([tile_of(w_ref, slots[block * keep + k]) for k in range(keep)], axis=1)
        for j in range(out_ref.shape[0]):
            right = jnp.concatenate([t_ref[j, screen[block, k]] for k in range(keep)], axis=0)
            here = slice(a * tile, (a + 1) * tile)
            out_ref[j, here, :] = near_ref[j, here, :].astype(F32) + jnp.dot(
                left, right, preferred_element_type=F32
            )


def final_kernel(slab, pair, place, occ_ref, base_ref, cycle_ref, va_ref, vb_ref, out_ref):
    rows = base_ref.shape[1]
    energy_a = jnp.broadcast_to(va_ref[...], (128, rows)).T[:, :1]
    pairs = energy_a + vb_ref[...]
    for j in range(base_ref.shape[0]):
        below = (pairs - occ_ref[slab[place[0]]]) - occ_ref[pair[j]]
        value = base_ref[j] + cycle_ref[0, j].astype(F32)
        out_ref[j] = (value / below).astype(BF16)


def body(
    amplitudes,
    coulomb,
    ladder_tiles,
    cycle_tiles,
    ladder_screen,
    tile_slot,
    cycle_screen,
    cycle_rows,
    cycle_count,
    slab_occ,
    window_occ,
    occ_energy,
    vir_energy,
):
    occ_count, vir_count = lax.axis_size("occ"), lax.axis_size("vir")
    _, window, width_all, block_cols = amplitudes.shape
    stored, tile, _ = ladder_tiles.shape
    tile_count = width_all // tile
    rows_here = width_all // vir_count
    share = stored // occ_count
    occ_at, vir_at = lax.axis_index("occ"), lax.axis_index("vir")
    place = jnp.stack([occ_at, vir_at]).astype(jnp.int32)
    t = amplitudes[0]
    near = coulomb[0]

    def gather(tiles):
        mine = lax.dynamic_slice_in_dim(tiles, occ_at * share, share, 0)
        full = lax.all_gather(mine, ("occ", "vir"), axis=0, tiled=True)
        return full.reshape(occ_count, vir_count, share, tile, tile)

    all_cycle = gather(cycle_tiles)
    all_ladder = gather(ladder_tiles)
    flat = t.reshape(window, vir_count, rows_here, block_cols).transpose(1, 0, 2, 3)
    moved = lax.all_to_all(flat, "vir", 0, 0, tiled=True)

    resident = lambda *shape: pl.BlockSpec(shape, lambda *_: (0,) * len(shape))
    step_block = pl.BlockSpec((window, rows_here, block_cols), lambda g, *_: (0, g, 0))
    swap_block = pl.BlockSpec((1, window, rows_here, block_cols), lambda g, *_: (g, 0, 0, 0))
    limit = pltpu.CompilerParams(vmem_limit_bytes=48 << 20)
    part = pl.pallas_call(
        cycle_kernel,
        out_shape=jax.ShapeDtypeStruct(moved.shape, BF16),
        grid_spec=pltpu.PrefetchScalarGridSpec(
            num_scalar_prefetch=4,
            grid=(vir_count,),
            in_specs=[resident(*moved.shape), resident(*all_cycle.shape)],
            out_specs=swap_block,
            scratch_shapes=[pltpu.SMEM((rows_here // tile, window * tile_count), jnp.int32)],
        ),
        compiler_params=limit,
    )(cycle_screen, cycle_rows, cycle_count, place, moved, all_cycle)
    cycle = lax.all_to_all(part, "vir", 0, 0, tiled=True)

    base = pl.pallas_call(
        ladder_kernel,
        out_shape=jax.ShapeDtypeStruct(t.shape, F32),
        grid_spec=pltpu.PrefetchScalarGridSpec(
            num_scalar_prefetch=2,
            grid=(vir_count,),
            in_specs=[
                resident(window, tile_count, tile, block_cols),
                resident(*all_ladder.shape),
                step_block,
            ],
            out_specs=step_block,
        ),
        compiler_params=limit,
    )(ladder_screen, tile_slot, t.reshape(window, tile_count, tile, block_cols), all_ladder, near)

    energies = vir_energy.reshape(1, width_all)
    out = pl.pallas_call(
        final_kernel,
        out_shape=jax.ShapeDtypeStruct(t.shape, BF16),
        grid_spec=pltpu.PrefetchScalarGridSpec(
            num_scalar_prefetch=3,
            grid=(vir_count,),
            in_specs=[
                pl.BlockSpec(memory_space=pltpu.SMEM),
                step_block,
                swap_block,
                pl.BlockSpec((1, rows_here), lambda g, *_: (0, g)),
                pl.BlockSpec((1, block_cols), lambda g, slab, pair, place: (0, place[1])),
            ],
            out_specs=step_block,
        ),
        compiler_params=limit,
    )(slab_occ, window_occ, place, occ_energy, base, cycle, energies, energies)
    return out[None]


def solution(mesh):
    wide = P("occ", None, None, "vir")
    tiles = P("vir", None, None)
    return jax.shard_map(
        body,
        mesh=mesh,
        in_specs=(wide, wide, tiles, tiles) + (P(),) * 9,
        out_specs=wide,
        check_vma=False,
    )
```

```python
import jax
import jax.numpy as jnp
from jax import lax
from jax.experimental import pallas as pl
from jax.experimental.pallas import tpu as pltpu
from jax.sharding import PartitionSpec as P

F32 = jnp.float32
BF16 = jnp.bfloat16
ANY = pl.BlockSpec(memory_space=pl.ANY)


def tile_of(ref, slot, x):
    xs, cores, _, share = ref.shape[:4]
    within = slot % (xs * cores * share)
    ahead = (within // (cores * share) - x) & (xs - 1)
    return ref[ahead, (within // share) % cores, slot // (xs * cores * share), within % share]


def load_tiles(place, mine, swapped, buf, sem):
    copies = []
    core = place[0] & 1
    for pieces, at in ((mine, core), (swapped, 1 - core)):
        near, behind, ahead, far_low, far_high = pieces
        half = far_low.shape[0]
        for src, dst in (
            (near, buf.at[0, at]),
            (ahead, buf.at[1, at]),
            (behind, buf.at[3, at]),
            (far_low, buf.at[2, at, pl.ds(0, half)]),
            (far_high, buf.at[2, at, pl.ds(half, half)]),
        ):
            copies.append(pltpu.make_async_copy(src, dst, sem.at[len(copies)]))
    for copy in copies:
        copy.start()
    return copies


def cycle_kernel(screen, rows, count, place, t_hbm, *refs):
    mine, swapped, (out_ref, mask, t_ref, z_ref, sem, t_sem) = refs[:5], refs[5:10], refs[10:]
    step = pl.program_id(0)
    tile = z_ref.shape[-1]
    height, width = t_ref.shape[2:]
    tiles_here, tiles_wide = height // tile, width // tile
    window, keep = t_ref.shape[1], screen.shape[1]
    tile_count = screen.shape[0] // window
    first = place[1] * tiles_here
    x = place[0] // 2

    @pl.when(step == 0)
    def _():
        copies = load_tiles(place, mine, swapped, z_ref, sem)
        copies.append(pltpu.make_async_copy(t_hbm, t_ref, t_sem))
        copies[-1].start()
        for a in range(tiles_here):

            @pl.loop(0, mask.shape[1])
            def _(q):
                mask[a, q] = 0

            @pl.loop(0, count[first + a])
            def _(e):
                mask[a, rows[first + a, e]] = 1

        for copy in copies:
            copy.wait()

    for j in range(window):
        for b in range(tiles_wide):
            q = j * tile_count + step * tiles_wide + b
            left, right = [], []
            for m in range(keep):
                u = screen[q, m]
                c = u % tile_count
                lane = pl.multiple_of((c % tiles_wide) * tile, tile)
                left.append(t_ref[c // tiles_wide, u // tile_count, :, pl.ds(lane, tile)])
                right.append(tile_of(z_ref, q * keep + m, x))
            part = jnp.dot(
                jnp.concatenate(left, axis=1),
                jnp.concatenate(right, axis=0),
                preferred_element_type=F32,
            )
            for a in range(tiles_here):
                rows_a = part[a * tile : (a + 1) * tile]
                used = jnp.full(rows_a.shape, mask[a, q], jnp.int32) > 0
                out_ref[0, j, a * tile : (a + 1) * tile, b * tile : (b + 1) * tile] = jnp.where(
                    used, rows_a, 0.0
                ).astype(BF16)


def ladder_kernel(screen, slots, place, t_ref, near_ref, *refs):
    mine, swapped, (out_ref, w_ref, sem) = refs[:5], refs[5:10], refs[10:]
    step = pl.program_id(0)
    tile = w_ref.shape[-1]
    keep = screen.shape[1]
    group = out_ref.shape[1] // tile
    x = place[0] // 2

    @pl.when(step == 0)
    def _():
        for copy in load_tiles(place, mine, swapped, w_ref, sem):
            copy.wait()

    for a in range(group):
        block = step * group + a
        left = jnp.concatenate(
            [tile_of(w_ref, slots[block * keep + k], x) for k in range(keep)], axis=1
        )
        for j in range(out_ref.shape[0]):
            right = jnp.concatenate([t_ref[j, screen[block, k]] for k in range(keep)], axis=0)
            here = slice(a * tile, (a + 1) * tile)
            out_ref[j, here, :] = near_ref[j, here, :].astype(F32) + jnp.dot(
                left, right, preferred_element_type=F32
            )


def final_kernel(slab, pair, place, occ_ref, base_ref, cycle_ref, va_ref, vb_ref, out_ref):
    rows = base_ref.shape[1]
    energy_a = jnp.broadcast_to(va_ref[...], (128, rows)).T[:, :1]
    pairs = energy_a + vb_ref[...]
    for j in range(base_ref.shape[0]):
        below = (pairs - occ_ref[slab[place[0]]]) - occ_ref[pair[j]]
        value = base_ref[j] + cycle_ref[0, j].astype(F32)
        out_ref[j] = (value / below).astype(BF16)


def body(
    amplitudes,
    coulomb,
    ladder_tiles,
    cycle_tiles,
    ladder_screen,
    tile_slot,
    cycle_screen,
    cycle_rows,
    cycle_count,
    slab_occ,
    window_occ,
    occ_energy,
    vir_energy,
):
    occ_count, vir_count = lax.axis_size("occ"), lax.axis_size("vir")
    _, window, width_all, block_cols = amplitudes.shape
    stored, tile, _ = ladder_tiles.shape
    tile_count = width_all // tile
    rows_here = width_all // vir_count
    share = stored // occ_count
    xs, zs = occ_count // 2, 4
    occ_at, vir_at = lax.axis_index("occ"), lax.axis_index("vir")
    place = jnp.stack([occ_at, vir_at]).astype(jnp.int32)
    t = amplitudes[0]
    near = coulomb[0]

    def occ_shift(value, by):
        return lax.ppermute(value, "occ", [(i, (i + 2 * by) % occ_count) for i in range(occ_count)])

    def core_swap(value):
        return lax.ppermute(value, "occ", [(i, i ^ 1) for i in range(occ_count)])

    def vir_shift(value, dy, dz):
        ys = vir_count // zs
        return lax.ppermute(
            value,
            "vir",
            [(y * zs + z, (y + dy) % ys * zs + (z + dz) % zs) for y in range(ys) for z in range(zs)],
        )

    def spread(piece):
        half = vir_count // 2
        behind, ahead = occ_shift(piece, 1), occ_shift(piece, -1)
        far_low, far_high = occ_shift(behind[:half], 1), occ_shift(ahead[half:], -1)
        mine = (piece, behind, ahead, far_low, far_high)
        return mine + tuple(core_swap(p) for p in mine)

    def my_share(tiles):
        return lax.dynamic_slice_in_dim(tiles, occ_at * share, share, 0)

    sent = jnp.broadcast_to(my_share(cycle_tiles)[None], (vir_count, share, tile, tile))
    cycle_piece = lax.all_to_all(sent, "vir", 0, 0, tiled=True)
    flat = t.reshape(window, vir_count, rows_here, block_cols).transpose(1, 0, 2, 3)
    flat, cycle_piece, ladder_share = lax.optimization_barrier(
        (flat, cycle_piece, my_share(ladder_tiles))
    )
    moved = lax.all_to_all(flat, "vir", 0, 0, tiled=True)
    cycle_parts = spread(cycle_piece)

    line = jnp.stack([ladder_share] + [vir_shift(ladder_share, 0, d) for d in range(1, zs)])
    plane = jnp.stack([line] + [vir_shift(line, d, 0) for d in range(1, vir_count // zs)])
    y, z = vir_at // zs, vir_at % zs
    plane = jnp.roll(jnp.flip(plane, (0, 1)), (y + 1, z + 1), (0, 1))
    ladder_piece = plane.reshape(vir_count, share, tile, tile)
    ladder_piece, *cycle_parts = lax.optimization_barrier((ladder_piece, *cycle_parts))
    ladder_parts = spread(ladder_piece)

    resident = lambda *shape: pl.BlockSpec(shape, lambda *_: (0,) * len(shape))
    step_block = pl.BlockSpec((window, rows_here, block_cols), lambda g, *_: (0, g, 0))
    swap_block = pl.BlockSpec((1, window, rows_here, block_cols), lambda g, *_: (g, 0, 0, 0))
    tile_buf = pltpu.VMEM((xs, 2, vir_count, share, tile, tile), BF16)
    tile_sem = pltpu.SemaphoreType.DMA((10,))
    limit = pltpu.CompilerParams(vmem_limit_bytes=48 << 20)
    part = pl.pallas_call(
        cycle_kernel,
        out_shape=jax.ShapeDtypeStruct(moved.shape, BF16),
        grid_spec=pltpu.PrefetchScalarGridSpec(
            num_scalar_prefetch=4,
            grid=(vir_count,),
            in_specs=[ANY] * 11,
            out_specs=swap_block,
            scratch_shapes=[
                pltpu.SMEM((rows_here // tile, window * tile_count), jnp.int32),
                pltpu.VMEM(moved.shape, BF16),
                tile_buf,
                tile_sem,
                pltpu.SemaphoreType.DMA(()),
            ],
        ),
        compiler_params=limit,
    )(cycle_screen, cycle_rows, cycle_count, place, moved, *cycle_parts)
    cycle = lax.all_to_all(part, "vir", 0, 0, tiled=True)

    base = pl.pallas_call(
        ladder_kernel,
        out_shape=jax.ShapeDtypeStruct(t.shape, F32),
        grid_spec=pltpu.PrefetchScalarGridSpec(
            num_scalar_prefetch=3,
            grid=(vir_count,),
            in_specs=[resident(window, tile_count, tile, block_cols), step_block] + [ANY] * 10,
            out_specs=step_block,
            scratch_shapes=[tile_buf, tile_sem],
        ),
        compiler_params=limit,
    )(
        ladder_screen,
        tile_slot,
        place,
        t.reshape(window, tile_count, tile, block_cols),
        near,
        *ladder_parts,
    )

    energies = vir_energy.reshape(1, width_all)
    out = pl.pallas_call(
        final_kernel,
        out_shape=jax.ShapeDtypeStruct(t.shape, BF16),
        grid_spec=pltpu.PrefetchScalarGridSpec(
            num_scalar_prefetch=3,
            grid=(vir_count,),
            in_specs=[
                pl.BlockSpec(memory_space=pltpu.SMEM),
                step_block,
                swap_block,
                pl.BlockSpec((1, rows_here), lambda g, *_: (0, g)),
                pl.BlockSpec((1, block_cols), lambda g, slab, pair, place: (0, place[1])),
            ],
            out_specs=step_block,
        ),
        compiler_params=limit,
    )(slab_occ, window_occ, place, occ_energy, base, cycle, energies, energies)
    return out[None]


def solution(mesh):
    wide = P("occ", None, None, "vir")
    tiles = P("vir", None, None)
    return jax.shard_map(
        body,
        mesh=mesh,
        in_specs=(wide, wide, tiles, tiles) + (P(),) * 9,
        out_specs=wide,
        check_vma=False,
    )
```

```python
import jax
import jax.numpy as jnp
from jax import lax
from jax.experimental import pallas as pl
from jax.experimental.pallas import tpu as pltpu
from jax.sharding import PartitionSpec as P

F32 = jnp.float32
BF16 = jnp.bfloat16
ANY = pl.BlockSpec(memory_space=pl.ANY)


SCALARS = pl.BlockSpec(memory_space=pltpu.SMEM)
FULL_VMEM = pltpu.CompilerParams(vmem_limit_bytes=60 << 20)


def tile_copies(place, pieces, buf, sem):
    xs = buf.shape[1]
    core, x = place[0] & 1, place[0] // 2
    groups = [[], [], [], []]
    for side, at in ((pieces[:5], core), (pieces[5:], 1 - core)):
        near, behind, ahead, far_low, far_high = side
        half = far_low.shape[0]
        whole = slice(None)
        for src, group, shift, where in (
            (near, 0, 0, whole),
            (behind, 1, xs - 1, whole),
            (ahead, 2, 1, whole),
            (far_low, 3, 2, pl.ds(0, half)),
            (far_high, 3, 2, pl.ds(half, half)),
        ):
            dst = buf.at[where, (x + shift) & (xs - 1), at]
            count = sum(map(len, groups))
            groups[group].append(pltpu.make_async_copy(src, dst, sem.at[count]))
    return groups


def chunk_copies(src, dst, sem):
    chunk = dst.shape[0] // sem.shape[0]
    return [
        pltpu.make_async_copy(src.at[pl.ds(i * chunk, chunk)], dst.at[pl.ds(i * chunk, chunk)], sem.at[i])
        for i in range(sem.shape[0])
    ]


def cycle_kernel(screen, rows, count, place, t_hbm, *refs):
    pieces, (out_hbm, mask, t_ref, z_ref, o_ref, t_sem, z_sem, o_sem) = refs[:10], refs[10:]
    keep, tile = screen.shape[1], z_ref.shape[-1]
    parts, window, height, width = t_ref.shape
    tiles_here, tiles_wide = height // tile, width // tile
    tile_count = screen.shape[0] // window
    vir, xs = z_ref.shape[:2]
    first = place[1] * tiles_here
    moves = chunk_copies(t_hbm, t_ref, t_sem)
    groups = tile_copies(place, pieces, z_ref, z_sem)
    for copy in moves + sum(groups, []):
        copy.start()
    for a in range(tiles_here):

        @pl.loop(0, mask.shape[1])
        def _(q):
            mask[a, q] = 0

        @pl.loop(0, count[first + a])
        def _(e):
            mask[a, rows[first + a, e]] = 1

    for copy in moves:
        copy.wait()

    def one(v, x):
        q = v * xs + x
        j, c_out = q // tile_count, q % tile_count
        step, lane_out = c_out // tiles_wide, c_out % tiles_wide
        left = []
        for m in range(keep):
            u = screen[q, m]
            c = u % tile_count
            lane = pl.multiple_of((c % tiles_wide) * tile, tile)
            left.append(t_ref[c // tiles_wide, u // tile_count, :, pl.ds(lane, tile)])
        right = z_ref[v, x].reshape(keep * tile, tile)
        part = jnp.dot(jnp.concatenate(left, axis=1), right, preferred_element_type=F32)
        for a in range(tiles_here):
            here = slice(a * tile, (a + 1) * tile)
            used = jnp.full((tile, tile), mask[a, q], jnp.int32) > 0
            lanes = pl.ds(pl.multiple_of(lane_out * tile, tile), tile)
            o_ref[step, j, here, lanes] = jnp.where(used, part[here], 0.0).astype(BF16)

    unroll = 4
    for group, shift in zip(groups, (0, xs - 1, 1, 2), strict=True):
        for copy in group:
            copy.wait()
        x = (place[0] // 2 + shift) & (xs - 1)

        @pl.loop(0, vir // unroll)
        def _(outer):
            for inner in range(unroll):
                one(outer * unroll + inner, x)

    out = pltpu.make_async_copy(o_ref, out_hbm, o_sem)
    out.start()
    out.wait()


def ladder_kernel(screen, slots, place, t_hbm, near_hbm, *refs):
    pieces, (out_hbm, t_ref, near_ref, w_ref, out_ref, t_sem, near_sem, w_sem, o_sem) = (
        refs[:10],
        refs[10:],
    )
    keep = screen.shape[1]
    window, blocks, tile, _ = t_ref.shape
    per_dev = w_ref.shape[1] * w_ref.shape[2] * w_ref.shape[3]
    share = w_ref.shape[3]
    copies = sum(tile_copies(place, pieces, w_ref, w_sem), []) + chunk_copies(t_hbm, t_ref, t_sem)
    copies += chunk_copies(near_hbm, near_ref, near_sem)
    for copy in copies:
        copy.start()
    for copy in copies:
        copy.wait()

    def one(block):
        tiles = []
        for k in range(keep):
            slot = slots[block * keep + k]
            within = slot % per_dev
            tiles.append(
                w_ref[slot // per_dev, within // (2 * share), (within // share) % 2, within % share]
            )
        left = jnp.concatenate(tiles, axis=1)
        for j in range(window):
            right = jnp.concatenate([t_ref[j, screen[block, k]] for k in range(keep)], axis=0)
            out_ref[j, block] = near_ref[j, block].astype(F32) + jnp.dot(
                left, right, preferred_element_type=F32
            )

    unroll = 2
    quarter = blocks // 4
    for part in range(4):

        @pl.loop(0, quarter // unroll)
        def _(outer):
            for inner in range(unroll):
                one(part * quarter + outer * unroll + inner)

        where = pl.ds(part * quarter, quarter)
        pltpu.make_async_copy(out_ref.at[:, where], out_hbm.at[:, where], o_sem.at[part]).start()
    for part in range(4):
        where = pl.ds(part * quarter, quarter)
        pltpu.make_async_copy(out_ref.at[:, where], out_hbm.at[:, where], o_sem.at[part]).wait()


def final_kernel(slab, pair, place, occ_ref, base_ref, cycle_ref, va_ref, vb_ref, out_ref):
    group, window, rows, cols = cycle_ref.shape
    for g in range(group):
        here = slice(g * rows, (g + 1) * rows)
        energy_a = jnp.broadcast_to(va_ref[:, here], (128, rows)).T
        pairs = jnp.concatenate([energy_a] * (cols // 128), axis=1) + vb_ref[...]
        for j in range(window):
            below = (pairs - occ_ref[slab[place[0]]]) - occ_ref[pair[j]]
            value = base_ref[j, here] + cycle_ref[g, j].astype(F32)
            out_ref[j, here] = (value / below).astype(BF16)


def body(
    amplitudes,
    coulomb,
    ladder_tiles,
    cycle_tiles,
    ladder_screen,
    tile_slot,
    cycle_screen,
    cycle_rows,
    cycle_count,
    slab_occ,
    window_occ,
    occ_energy,
    vir_energy,
):
    occ_count, vir_count = lax.axis_size("occ"), lax.axis_size("vir")
    _, window, width_all, block_cols = amplitudes.shape
    stored, tile, _ = ladder_tiles.shape
    tile_count = width_all // tile
    rows_here = width_all // vir_count
    share = stored // occ_count
    xs, zs = occ_count // 2, 4
    occ_at, vir_at = lax.axis_index("occ"), lax.axis_index("vir")
    place = jnp.stack([occ_at, vir_at]).astype(jnp.int32)
    t = amplitudes[0]
    near = coulomb[0]

    def occ_shift(value, by):
        return lax.ppermute(value, "occ", [(i, (i + 2 * by) % occ_count) for i in range(occ_count)])

    def core_swap(value):
        return lax.ppermute(value, "occ", [(i, i ^ 1) for i in range(occ_count)])

    def vir_shift(value, dy, dz):
        ys = vir_count // zs
        return lax.ppermute(
            value,
            "vir",
            [(y * zs + z, (y + dy) % ys * zs + (z + dz) % zs) for y in range(ys) for z in range(zs)],
        )

    def ring(value, shift):
        half = value.shape[0] // 2
        behind, ahead = shift(value, 1), shift(value, -1)
        far = jnp.concatenate([shift(behind[:half], 1), shift(ahead[half:], -1)])
        return jnp.stack([value, behind, far, ahead])

    def spread(piece):
        half = vir_count // 2
        behind, ahead = occ_shift(piece, 1), occ_shift(piece, -1)
        far_low, far_high = occ_shift(behind[:half], 1), occ_shift(ahead[half:], -1)
        mine = (piece, behind, ahead, far_low, far_high)
        return mine + tuple(core_swap(p) for p in mine)

    def my_share(tiles):
        return lax.dynamic_slice_in_dim(tiles, occ_at * share, share, 0)

    sent = jnp.broadcast_to(my_share(cycle_tiles)[None], (vir_count, share, tile, tile))
    cycle_piece = lax.all_to_all(sent, "vir", 0, 0, tiled=True)
    line = ring(my_share(ladder_tiles), lambda value, by: vir_shift(value, 0, by))
    plane = ring(line, lambda value, by: vir_shift(value, by, 0))
    flat = t.reshape(window, vir_count, rows_here, block_cols).transpose(1, 0, 2, 3)
    flat, cycle_piece, plane = lax.optimization_barrier((flat, cycle_piece, plane))
    moved = lax.all_to_all(flat, "vir", 0, 0, tiled=True)
    cycle_parts = spread(cycle_piece)

    y, z = vir_at // zs, vir_at % zs
    plane = jnp.roll(jnp.flip(plane, (0, 1)), (y + 1, z + 1), (0, 1))
    ladder_piece = plane.reshape(vir_count, share, tile, tile)
    ladder_piece, *_ = lax.optimization_barrier((ladder_piece, *cycle_parts[3:5]))
    ladder_parts = spread(ladder_piece)

    tile_buf = pltpu.VMEM((vir_count, xs, 2, share, tile, tile), BF16)
    dma = pltpu.SemaphoreType.DMA
    part = pl.pallas_call(
        cycle_kernel,
        out_shape=jax.ShapeDtypeStruct(moved.shape, BF16),
        grid_spec=pltpu.PrefetchScalarGridSpec(
            num_scalar_prefetch=4,
            grid=(1,),
            in_specs=[ANY] * 11,
            out_specs=ANY,
            scratch_shapes=[
                pltpu.SMEM((rows_here // tile, window * tile_count), jnp.int32),
                pltpu.VMEM(moved.shape, BF16),
                tile_buf,
                pltpu.VMEM(moved.shape, BF16),
                dma((2,)),
                dma((10,)),
                dma(()),
            ],
        ),
        compiler_params=FULL_VMEM,
    )(cycle_screen, cycle_rows, cycle_count, place, moved, *cycle_parts)
    cycle = lax.all_to_all(part, "vir", 0, 0, tiled=True)

    blocked = (window, tile_count, tile, block_cols)
    base = pl.pallas_call(
        ladder_kernel,
        out_shape=jax.ShapeDtypeStruct(blocked, F32),
        grid_spec=pltpu.PrefetchScalarGridSpec(
            num_scalar_prefetch=3,
            grid=(1,),
            in_specs=[ANY] * 12,
            out_specs=ANY,
            scratch_shapes=[
                pltpu.VMEM(blocked, BF16),
                pltpu.VMEM(blocked, BF16),
                tile_buf,
                pltpu.VMEM(blocked, F32),
                dma((2,)),
                dma((2,)),
                dma((10,)),
                dma((4,)),
            ],
        ),
        compiler_params=FULL_VMEM,
    )(ladder_screen, tile_slot, place, t.reshape(blocked), near.reshape(blocked), *ladder_parts)

    energies = vir_energy.reshape(1, width_all)
    group = 4
    out = pl.pallas_call(
        final_kernel,
        out_shape=jax.ShapeDtypeStruct(t.shape, BF16),
        grid_spec=pltpu.PrefetchScalarGridSpec(
            num_scalar_prefetch=3,
            grid=(vir_count // group,),
            in_specs=[
                SCALARS,
                pl.BlockSpec((window, group * rows_here, block_cols), lambda g, *_: (0, g, 0)),
                pl.BlockSpec((group, window, rows_here, block_cols), lambda g, *_: (g, 0, 0, 0)),
                pl.BlockSpec((1, group * rows_here), lambda g, *_: (0, g)),
                pl.BlockSpec((1, block_cols), lambda g, slab, pair, place: (0, place[1])),
            ],
            out_specs=pl.BlockSpec((window, group * rows_here, block_cols), lambda g, *_: (0, g, 0)),
        ),
        compiler_params=FULL_VMEM,
    )(
        slab_occ,
        window_occ,
        place,
        occ_energy,
        base.reshape(t.shape),
        cycle,
        energies,
        energies,
    )
    return out[None]


def solution(mesh):
    wide = P("occ", None, None, "vir")
    tiles = P("vir", None, None)
    return jax.shard_map(
        body,
        mesh=mesh,
        in_specs=(wide, wide, tiles, tiles) + (P(),) * 9,
        out_specs=wide,
        check_vma=False,
    )
```

```python
import functools

import jax
import jax.numpy as jnp
from jax import lax
from jax.experimental import pallas as pl
from jax.experimental.pallas import tpu as pltpu
from jax.sharding import PartitionSpec as P


F32 = jnp.float32
BF16 = jnp.bfloat16
ANY = pl.BlockSpec(memory_space=pl.ANY)


SCALARS = pl.BlockSpec(memory_space=pltpu.SMEM)
FULL_VMEM = pltpu.CompilerParams(vmem_limit_bytes=60 << 20)


def tile_copies(place, pieces, buf, sem):
    xs = buf.shape[1]
    core, x = place[0] & 1, place[0] // 2
    groups = [[], [], [], []]
    for side, at in ((pieces[:5], core), (pieces[5:], 1 - core)):
        near, behind, ahead, far_low, far_high = side
        half = far_low.shape[0]
        whole = slice(None)
        for src, group, shift, where in (
            (near, 0, 0, whole),
            (behind, 1, xs - 1, whole),
            (ahead, 2, 1, whole),
            (far_low, 3, 2, pl.ds(0, half)),
            (far_high, 3, 2, pl.ds(half, half)),
        ):
            dst = buf.at[where, (x + shift) & (xs - 1), at]
            count = sum(map(len, groups))
            groups[group].append(pltpu.make_async_copy(src, dst, sem.at[count]))
    return groups


def chunk_copies(src, dst, sem):
    chunk = dst.shape[0] // sem.shape[0]
    return [
        pltpu.make_async_copy(src.at[pl.ds(i * chunk, chunk)], dst.at[pl.ds(i * chunk, chunk)], sem.at[i])
        for i in range(sem.shape[0])
    ]


def cost(flops, bytes_accessed):
    return pl.CostEstimate(flops=flops, bytes_accessed=bytes_accessed, transcendentals=0)


def cycle_kernel(screen, rows, count, place, t_hbm, *refs, side):
    pieces, (out_hbm, t_ref, z_ref, o_ref, t_sem, z_sem, o_sem) = refs[:10], refs[10:]
    keep, tile = screen.shape[1], z_ref.shape[-1]
    parts, window, _, width = t_ref.shape
    tiles_wide = width // tile
    tile_count = screen.shape[0] // window
    xs = z_ref.shape[1]
    block = place[1] * (rows.shape[0] // parts) + side
    copies = chunk_copies(t_hbm, t_ref, t_sem) + sum(tile_copies(place, pieces, z_ref, z_sem), [])
    for copy in copies:
        copy.start()
    for part in range(parts):
        o_ref[part] = jnp.zeros(o_ref.shape[1:], BF16)
    for copy in copies:
        copy.wait()

    def one(entry):
        q = rows[block, entry]
        j, c_out = q // tile_count, q % tile_count
        left = []
        for m in range(keep):
            u = screen[q, m]
            c = u % tile_count
            lane = pl.multiple_of((c % tiles_wide) * tile, tile)
            left.append(t_ref[c // tiles_wide, u // tile_count, :, pl.ds(lane, tile)])
        right = z_ref[q // xs, q % xs].reshape(keep * tile, tile)
        part = jnp.dot(jnp.concatenate(left, axis=1), right, preferred_element_type=F32)
        lanes = pl.ds(pl.multiple_of((c_out % tiles_wide) * tile, tile), tile)
        o_ref[c_out // tiles_wide, j, :, lanes] = part.astype(BF16)

    used = count[block]
    unroll = 4

    @pl.loop(0, (used + unroll - 1) // unroll)
    def _(outer):
        for inner in range(unroll):
            one(jnp.minimum(outer * unroll + inner, used - 1))

    out = pltpu.make_async_copy(o_ref, out_hbm, o_sem)
    out.start()
    out.wait()


def ladder_kernel(screen, slots, place, t_hbm, near_hbm, *refs, side):
    pieces, (out_hbm, t_ref, near_ref, w_ref, out_ref, t_sem, near_sem, w_sem, o_sem) = (
        refs[:10],
        refs[10:],
    )
    keep = screen.shape[1]
    window, parts, _, _ = out_ref.shape
    sides = t_ref.shape[1] // parts
    share = w_ref.shape[3]
    per_dev = w_ref.shape[1] * w_ref.shape[2] * share
    copies = sum(tile_copies(place, pieces, w_ref, w_sem), []) + chunk_copies(t_hbm, t_ref, t_sem)
    copies.append(pltpu.make_async_copy(near_hbm.at[:, :, side], near_ref, near_sem))
    for copy in copies:
        copy.start()
    for copy in copies:
        copy.wait()

    def one(part):
        block = part * sides + side
        tiles = []
        for k in range(keep):
            slot = slots[block * keep + k]
            within = slot % per_dev
            tiles.append(
                w_ref[slot // per_dev, within // (2 * share), (within // share) % 2, within % share]
            )
        left = jnp.concatenate(tiles, axis=1)
        for j in range(window):
            right = jnp.concatenate([t_ref[j, screen[block, k]] for k in range(keep)], axis=0)
            out_ref[j, part] = near_ref[j, part].astype(F32) + jnp.dot(
                left, right, preferred_element_type=F32
            )

    unroll = 2
    chunks = o_sem.shape[0]
    size = parts // chunks

    def leave(chunk):
        where = pl.ds(chunk * size, size)
        return pltpu.make_async_copy(out_ref.at[:, where], out_hbm.at[:, where], o_sem.at[chunk])

    for chunk in range(chunks):

        @pl.loop(0, size // unroll)
        def _(outer):
            for inner in range(unroll):
                one(chunk * size + outer * unroll + inner)

        leave(chunk).start()
    for chunk in range(chunks):
        leave(chunk).wait()


def final_kernel(slab, pair, place, occ_ref, base_ref, cycle_ref, va_ref, vb_ref, *refs, side):
    out_ref = refs[-1]
    group, window, rows, cols = cycle_ref.shape
    sides = va_ref.shape[1] // (group * rows)
    for g in range(group):
        start = (g * sides + side) * rows
        energy_a = jnp.broadcast_to(va_ref[:, start : start + rows], (rows, rows)).T
        pairs = jnp.concatenate([energy_a] * (cols // rows), axis=1) + vb_ref[...]
        for j in range(window):
            below = (pairs - occ_ref[slab[place[0]]]) - occ_ref[pair[j]]
            value = base_ref[j, g] + cycle_ref[g, j].astype(F32)
            out_ref[j, g, 0] = (value / below).astype(BF16)


def body(
    amplitudes,
    coulomb,
    ladder_tiles,
    cycle_tiles,
    ladder_screen,
    tile_slot,
    cycle_screen,
    cycle_rows,
    cycle_count,
    slab_occ,
    window_occ,
    occ_energy,
    vir_energy,
):
    occ_count, vir_count = lax.axis_size("occ"), lax.axis_size("vir")
    _, window, width_all, block_cols = amplitudes.shape
    stored, tile, _ = ladder_tiles.shape
    tile_count = width_all // tile
    rows_here = width_all // vir_count
    share = stored // occ_count
    xs, zs = occ_count // 2, 4
    occ_at, vir_at = lax.axis_index("occ"), lax.axis_index("vir")
    place = jnp.stack([occ_at, vir_at]).astype(jnp.int32)
    t = amplitudes[0]
    near = coulomb[0]

    def occ_shift(value, by):
        return lax.ppermute(value, "occ", [(i, (i + 2 * by) % occ_count) for i in range(occ_count)])

    def core_swap(value):
        return lax.ppermute(value, "occ", [(i, i ^ 1) for i in range(occ_count)])

    def vir_shift(value, dy, dz):
        ys = vir_count // zs
        return lax.ppermute(
            value,
            "vir",
            [(y * zs + z, (y + dy) % ys * zs + (z + dz) % zs) for y in range(ys) for z in range(zs)],
        )

    def ring(value, shift, size):
        return jnp.stack([value] + [shift(value, d) for d in range(1, size)])

    def spread(piece):
        half = vir_count // 2
        behind, ahead = occ_shift(piece, 1), occ_shift(piece, -1)
        far_low, far_high = occ_shift(behind[:half], 1), occ_shift(ahead[half:], -1)
        mine = (piece, behind, ahead, far_low, far_high)
        return mine + tuple(core_swap(p) for p in mine)

    def my_share(tiles):
        return lax.dynamic_slice_in_dim(tiles, occ_at * share, share, 0)

    sent = jnp.broadcast_to(my_share(cycle_tiles)[None], (vir_count, share, tile, tile))
    cycle_piece = lax.all_to_all(sent, "vir", 0, 0, tiled=True)
    sides = rows_here // tile
    split = t.reshape(window, vir_count, sides, tile, block_cols)
    flats = [split[:, :, side].transpose(1, 0, 2, 3) for side in range(sides)]
    flats[0], ladder_share = lax.optimization_barrier((flats[0], my_share(ladder_tiles)))
    line = ring(ladder_share, lambda value, by: vir_shift(value, 0, by), zs)
    flats[0], cycle_piece, line = lax.optimization_barrier((flats[0], cycle_piece, line))
    plane = ring(line, lambda value, by: vir_shift(value, by, 0), vir_count // zs)
    moved = []
    for flat in flats:
        if moved:
            flat, moved[-1] = lax.optimization_barrier((flat, moved[-1]))
        moved.append(lax.all_to_all(flat, "vir", 0, 0, tiled=True))
    cycle_parts = spread(cycle_piece)

    plane, *_ = lax.optimization_barrier((plane, *cycle_parts))
    y, z = vir_at // zs, vir_at % zs
    plane = jnp.roll(jnp.flip(plane, (0, 1)), (y + 1, z + 1), (0, 1))
    ladder_parts = spread(plane.reshape(vir_count, share, tile, tile))

    tile_buf = pltpu.VMEM((vir_count, xs, 2, share, tile, tile), BF16)
    dma = pltpu.SemaphoreType.DMA
    half = (vir_count, window, tile, block_cols)
    size = vir_count * window * tile * block_cols
    tile_bytes = 2 * stored * vir_count * tile * tile

    def cycle_half(side):
        return pl.pallas_call(
            functools.partial(cycle_kernel, side=side),
            out_shape=pltpu.HBM(half, BF16),
            grid_spec=pltpu.PrefetchScalarGridSpec(
                num_scalar_prefetch=4,
                grid=(1,),
                in_specs=[ANY] * 11,
                out_specs=ANY,
                scratch_shapes=[
                    pltpu.VMEM(half, BF16),
                    tile_buf,
                    pltpu.VMEM(half, BF16),
                    dma((2,)),
                    dma((10,)),
                    dma(()),
                ],
            ),
            compiler_params=pltpu.CompilerParams(vmem_limit_bytes=16 << 20),
            cost_estimate=cost(8 * size * tile, 4 * size + tile_bytes),
        )(cycle_screen, cycle_rows, cycle_count, place, moved[side], *cycle_parts)

    blocked = (window, tile_count, tile, block_cols)
    base_shape = (window, vir_count, tile, block_cols)

    def base_half(side):
        return pl.pallas_call(
            functools.partial(ladder_kernel, side=side),
            out_shape=jax.ShapeDtypeStruct(base_shape, F32),
            grid_spec=pltpu.PrefetchScalarGridSpec(
                num_scalar_prefetch=3,
                grid=(1,),
                in_specs=[ANY] * 12,
                out_specs=ANY,
                scratch_shapes=[
                    pltpu.VMEM(blocked, BF16),
                    pltpu.VMEM(base_shape, BF16),
                    tile_buf,
                    pltpu.VMEM(base_shape, F32),
                    dma((2,)),
                    dma(()),
                    dma((10,)),
                    dma((4,)),
                ],
            ),
            compiler_params=FULL_VMEM,
            cost_estimate=cost(16 * size * tile, 10 * size + tile_bytes),
        )(
            ladder_screen,
            tile_slot,
            place,
            t.reshape(blocked),
            near.reshape(window, vir_count, sides, tile, block_cols),
            *ladder_parts,
        )

    energies = vir_energy.reshape(1, width_all)
    group = 4

    def final_half(side, base, cycle, out):
        old = [] if out is None else [out]
        return pl.pallas_call(
            functools.partial(final_kernel, side=side),
            out_shape=jax.ShapeDtypeStruct(split.shape, BF16),
            grid_spec=pltpu.PrefetchScalarGridSpec(
                num_scalar_prefetch=3,
                grid=(vir_count // group,),
                in_specs=[
                    SCALARS,
                    pl.BlockSpec((window, group, tile, block_cols), lambda g, *_: (0, g, 0, 0)),
                    pl.BlockSpec((group, window, tile, block_cols), lambda g, *_: (g, 0, 0, 0)),
                    pl.BlockSpec((1, group * rows_here), lambda g, *_: (0, g)),
                    pl.BlockSpec((1, block_cols), lambda g, slab, pair, place: (0, place[1])),
                ]
                + [ANY] * len(old),
                out_specs=pl.BlockSpec(
                    (window, group, 1, tile, block_cols), lambda g, *_: (0, g, side, 0, 0)
                ),
            ),
            compiler_params=pltpu.CompilerParams(vmem_limit_bytes=61 << 20),
            cost_estimate=cost(8 * size, 8 * size),
            input_output_aliases={8: 0} if old else {},
        )(slab_occ, window_occ, place, occ_energy, base, cycle, energies, energies, *old)

    back, bases, out = [], [], None
    for side in range(sides):
        part = cycle_half(side)
        if not back:
            part, _ = lax.optimization_barrier((part, moved[-1]))
        back.append(lax.all_to_all(part, "vir", 0, 0, tiled=True))
    for side in range(sides):
        bases.append(base_half(side))
    for side in range(sides):
        out = final_half(side, bases[side], back[side], out)
    return out.reshape(amplitudes.shape)


def solution(mesh):
    wide = P("occ", None, None, "vir")
    tiles = P("vir", None, None)
    return jax.shard_map(
        body,
        mesh=mesh,
        in_specs=(wide, wide, tiles, tiles) + (P(),) * 9,
        out_specs=wide,
        check_vma=False,
    )
```

```python
import jax
import jax.numpy as jnp
from jax import lax
from jax.experimental import pallas as pl
from jax.experimental.pallas import tpu as pltpu
from jax.sharding import PartitionSpec as P


F32 = jnp.float32
BF16 = jnp.bfloat16
ANY = pl.BlockSpec(memory_space=pl.ANY)
SCALARS = pl.BlockSpec(memory_space=pltpu.SMEM)


def room(mib):
    return pltpu.CompilerParams(vmem_limit_bytes=mib << 20)


def cost(flops, bytes_accessed):
    return pl.CostEstimate(flops=flops, bytes_accessed=bytes_accessed, transcendentals=0)


def tile_copies(place, pieces, buf, sem):
    xs = buf.shape[1]
    core, x = place[0] & 1, place[0] // 2
    groups = [[], [], [], []]
    half = buf.shape[0] // 2
    for side, at in ((pieces[:8], core), (pieces[8:], 1 - core)):
        for number, src in enumerate(side):
            group = number // 2
            dst = buf.at[pl.ds(number % 2 * half, half), (x + (0, xs - 1, 1, 2)[group]) & (xs - 1), at]
            count = sum(map(len, groups))
            groups[group].append(pltpu.make_async_copy(src, dst, sem.at[count]))
    return groups


def cycle_kernel(screen, rows, count, place, t_hbm, *refs):
    pieces, (out_hbm, mask, t_ref, z_ref, o_ref, t_sem, z_sem, o_sem) = refs[:16], refs[16:]
    keep, tile = screen.shape[1], z_ref.shape[-1]
    _, window, height, width = t_ref.shape
    tiles_here, tiles_wide = height // tile, width // tile
    tile_count = screen.shape[0] // window
    vir, xs = z_ref.shape[:2]
    first = place[1] * tiles_here
    moves = [pltpu.make_async_copy(t_hbm, t_ref, t_sem)]
    groups = tile_copies(place, pieces, z_ref, z_sem)
    for copy in moves + sum(groups, []):
        copy.start()
    for a in range(tiles_here):

        @pl.loop(0, mask.shape[1])
        def _(q):
            mask[a, q] = 0

        @pl.loop(0, count[first + a])
        def _(e):
            mask[a, rows[first + a, e]] = 1

    for copy in moves:
        copy.wait()

    pairs = o_ref.shape[1]

    def one(v, x):
        q = v * xs + x
        left = []
        for m in range(keep):
            u = screen[q, m]
            c = u % tile_count
            lane = pl.multiple_of((c % tiles_wide) * tile, tile)
            left.append(t_ref[c // tiles_wide, u // tile_count, :, pl.ds(lane, tile)])
        right = z_ref[v, x].reshape(keep * tile, tile)
        part = jnp.dot(jnp.concatenate(left, axis=1), right, preferred_element_type=F32)
        for a in range(tiles_here):
            here = slice(a * tile, (a + 1) * tile)
            used = jnp.full((tile, tile), mask[a, q], jnp.int32) > 0
            o_ref[x, v % pairs, v // pairs, here] = jnp.where(used, part[here], 0.0).astype(BF16)

    unroll = 16
    leaves = []
    for group, shift in zip(groups, (0, xs - 1, 1, 2), strict=True):
        for copy in group:
            copy.wait()
        x = (place[0] // 2 + shift) & (xs - 1)

        @pl.loop(0, vir // unroll)
        def _(outer):
            for inner in range(unroll):
                one(outer * unroll + inner, x)

        lanes = pl.ds(pl.multiple_of((x % tiles_wide) * tile, tile), tile)
        there = out_hbm.at[:, x // tiles_wide, :, :, lanes]
        leaves.append(pltpu.make_async_copy(o_ref.at[x], there, o_sem.at[len(leaves)]))
        leaves[-1].start()
    for copy in leaves:
        copy.wait()


def ladder_kernel(screen, slots, place, t_hbm, near_hbm, *refs):
    pieces, (out_hbm, t_ref, near_ref, w_ref, out_ref, t_sem, near_sem, w_sem, o_sem) = (
        refs[:16],
        refs[16:],
    )
    keep = screen.shape[1]
    window, blocks, _, _ = t_ref.shape
    vir, xs, cores, share = w_ref.shape[:4]
    zs = vir // xs
    per_dev = xs * cores * share
    chunks = o_sem.shape[0]
    size = blocks // chunks
    copies = sum(tile_copies(place, pieces, w_ref, w_sem), [])
    copies.append(pltpu.make_async_copy(t_hbm, t_ref, t_sem))

    def arrive(chunk):
        where = pl.ds(chunk * size, size)
        return pltpu.make_async_copy(
            near_hbm.at[:, where], near_ref.at[:, where], near_sem.at[chunk]
        )

    for copy in copies + [arrive(chunk) for chunk in range(chunks)]:
        copy.start()
    y, z = place[1] // zs, place[1] % zs
    for copy in copies:
        copy.wait()

    def one(block):
        tiles = []
        for k in range(keep):
            slot = slots[block * keep + k]
            v, within = slot // per_dev, slot % per_dev
            behind = ((y - v // zs) & (zs - 1)) * zs + ((z - v % zs) & (zs - 1))
            tiles.append(
                w_ref[behind, within // (cores * share), (within // share) % cores, within % share]
            )
        left = jnp.concatenate(tiles, axis=1)
        for j in range(window):
            right = jnp.concatenate([t_ref[j, screen[block, k]] for k in range(keep)], axis=0)
            out_ref[j, block] = near_ref[j, block].astype(F32) + jnp.dot(
                left, right, preferred_element_type=F32
            )

    unroll = 4

    def leave(chunk):
        where = pl.ds(chunk * size, size)
        return pltpu.make_async_copy(out_ref.at[:, where], out_hbm.at[:, where], o_sem.at[chunk])

    for chunk in range(chunks):
        arrive(chunk).wait()

        @pl.loop(0, size // unroll)
        def _(outer):
            for inner in range(unroll):
                one(chunk * size + outer * unroll + inner)

        leave(chunk).start()
    for chunk in range(chunks):
        leave(chunk).wait()


def final_kernel(slab, pair, place, occ_ref, base_ref, cycle_ref, va_ref, vb_ref, out_ref):
    group, window, rows, cols = cycle_ref.shape
    for g in range(group):
        here = slice(g * rows, (g + 1) * rows)
        energy_a = jnp.broadcast_to(va_ref[:, here], (128, rows)).T
        pairs = jnp.concatenate([energy_a] * (cols // 128), axis=1) + vb_ref[...]
        for j in range(window):
            below = (pairs - occ_ref[slab[place[0]]]) - occ_ref[pair[j]]
            value = base_ref[j, here] + cycle_ref[g, j].astype(F32)
            out_ref[j, here] = (value / below).astype(BF16)


def body(
    amplitudes,
    coulomb,
    ladder_tiles,
    cycle_tiles,
    ladder_screen,
    tile_slot,
    cycle_screen,
    cycle_rows,
    cycle_count,
    slab_occ,
    window_occ,
    occ_energy,
    vir_energy,
):
    occ_count, vir_count = lax.axis_size("occ"), lax.axis_size("vir")
    _, window, width_all, block_cols = amplitudes.shape
    stored, tile, _ = ladder_tiles.shape
    tile_count = width_all // tile
    rows_here = width_all // vir_count
    share = stored // occ_count
    xs, zs = occ_count // 2, 4
    occ_at, vir_at = lax.axis_index("occ"), lax.axis_index("vir")
    place = jnp.stack([occ_at, vir_at]).astype(jnp.int32)
    t = amplitudes[0]
    near = coulomb[0]

    def occ_shift(value, by):
        return lax.ppermute(value, "occ", [(i, (i + 2 * by) % occ_count) for i in range(occ_count)])

    def core_swap(value):
        return lax.ppermute(value, "occ", [(i, i ^ 1) for i in range(occ_count)])

    def vir_shift(value, dy, dz):
        ys = vir_count // zs
        return lax.ppermute(
            value,
            "vir",
            [(y * zs + z, (y + dy) % ys * zs + (z + dz) % zs) for y in range(ys) for z in range(zs)],
        )

    def ring(value, shift, size):
        return jnp.stack([value] + [shift(value, d) for d in range(1, size)])

    def spread(piece):
        half = vir_count // 2
        low, high = piece[:half], piece[half:]
        behind_low, ahead_high = occ_shift(low, 1), occ_shift(high, -1)
        behind_high, ahead_low = occ_shift(high, 1), occ_shift(low, -1)
        far_low, far_high = occ_shift(behind_low, 1), occ_shift(ahead_high, -1)
        mine = (low, high, behind_low, behind_high, ahead_low, ahead_high, far_low, far_high)
        return mine + tuple(core_swap(p) for p in mine)

    def my_share(tiles):
        return lax.dynamic_slice_in_dim(tiles, occ_at * share, share, 0)

    sent = jnp.broadcast_to(my_share(cycle_tiles)[None], (vir_count, share, tile, tile))
    cycle_piece = lax.all_to_all(sent, "vir", 0, 0, tiled=True)
    flat = t.reshape(window, vir_count, rows_here, block_cols).transpose(1, 0, 2, 3)
    line = ring(my_share(ladder_tiles), lambda value, by: vir_shift(value, 0, by), zs)
    flat, cycle_piece, line = lax.optimization_barrier((flat, cycle_piece, line))
    plane = ring(line, lambda value, by: vir_shift(value, by, 0), vir_count // zs)
    moved = lax.all_to_all(flat, "vir", 0, 0, tiled=True)
    cycle_parts = spread(cycle_piece)

    tile_buf = pltpu.VMEM((vir_count, xs, 2, share, tile, tile), BF16)
    dma = pltpu.SemaphoreType.DMA
    size = window * width_all * block_cols
    tile_bytes = 2 * stored * vir_count * tile * tile
    whole = (vir_count, window, rows_here, block_cols)
    paired = (vir_count // 2, 2, window, rows_here, block_cols)
    part = pl.pallas_call(
        cycle_kernel,
        out_shape=pltpu.HBM(paired, BF16),
        grid_spec=pltpu.PrefetchScalarGridSpec(
            num_scalar_prefetch=4,
            grid=(1,),
            in_specs=[ANY] * 17,
            out_specs=ANY,
            scratch_shapes=[
                pltpu.SMEM((rows_here // tile, window * tile_count), jnp.int32),
                pltpu.VMEM(whole, BF16),
                tile_buf,
                pltpu.VMEM((xs, vir_count // 2, window, rows_here, tile), BF16),
                dma(()),
                dma((16,)),
                dma((4,)),
            ],
        ),
        compiler_params=room(60),
        cost_estimate=cost(8 * size * tile, 4 * size + tile_bytes),
    )(cycle_screen, cycle_rows, cycle_count, place, moved, *cycle_parts)
    cycle = lax.all_to_all(part.reshape(whole), "vir", 0, 0, tiled=True)

    ladder_parts = spread(plane.reshape(vir_count, share, tile, tile))
    blocked = (window, tile_count, tile, block_cols)
    base = pl.pallas_call(
        ladder_kernel,
        out_shape=pltpu.HBM(blocked, F32),
        grid_spec=pltpu.PrefetchScalarGridSpec(
            num_scalar_prefetch=3,
            grid=(1,),
            in_specs=[ANY] * 18,
            out_specs=ANY,
            scratch_shapes=[
                pltpu.VMEM(blocked, BF16),
                pltpu.VMEM(blocked, BF16),
                tile_buf,
                pltpu.VMEM(blocked, F32),
                dma(()),
                dma((4,)),
                dma((16,)),
                dma((4,)),
            ],
        ),
        compiler_params=room(60),
        cost_estimate=cost(16 * size * tile, 8 * size + tile_bytes),
    )(ladder_screen, tile_slot, place, t.reshape(blocked), near.reshape(blocked), *ladder_parts)

    energies = vir_energy.reshape(1, width_all)
    group = 4
    out = pl.pallas_call(
        final_kernel,
        out_shape=jax.ShapeDtypeStruct(t.shape, BF16),
        grid_spec=pltpu.PrefetchScalarGridSpec(
            num_scalar_prefetch=3,
            grid=(vir_count // group,),
            in_specs=[
                SCALARS,
                pl.BlockSpec((window, group * rows_here, block_cols), lambda g, *_: (0, g, 0)),
                pl.BlockSpec((group, window, rows_here, block_cols), lambda g, *_: (g, 0, 0, 0)),
                pl.BlockSpec((1, group * rows_here), lambda g, *_: (0, g)),
                pl.BlockSpec((1, block_cols), lambda g, slab, pair, place: (0, place[1])),
            ],
            out_specs=pl.BlockSpec(
                (window, group * rows_here, block_cols), lambda g, *_: (0, g, 0)
            ),
        ),
        compiler_params=room(60),
        cost_estimate=cost(8 * size, 8 * size),
    )(
        slab_occ,
        window_occ,
        place,
        occ_energy,
        base.reshape(t.shape),
        cycle,
        energies,
        energies,
    )
    return out[None]


def solution(mesh):
    wide = P("occ", None, None, "vir")
    tiles = P("vir", None, None)
    return jax.shard_map(
        body,
        mesh=mesh,
        in_specs=(wide, wide, tiles, tiles) + (P(),) * 9,
        out_specs=wide,
        check_vma=False,
    )
```

```python
import jax
import jax.numpy as jnp
from jax import lax
from jax.experimental import pallas as pl
from jax.experimental.pallas import tpu as pltpu
from jax.sharding import PartitionSpec as P


F32 = jnp.float32
BF16 = jnp.bfloat16
ANY = pl.BlockSpec(memory_space=pl.ANY)
SCALARS = pl.BlockSpec(memory_space=pltpu.SMEM)


def room(mib):
    return pltpu.CompilerParams(vmem_limit_bytes=mib << 20)


def cost(flops, bytes_accessed):
    return pl.CostEstimate(flops=flops, bytes_accessed=bytes_accessed, transcendentals=0)


def tile_copies(place, pieces, buf, sem):
    xs = buf.shape[1]
    core, x = place[0] & 1, place[0] // 2
    groups = [[], [], [], []]
    half = buf.shape[0] // 2
    for side, at in ((pieces[:8], core), (pieces[8:], 1 - core)):
        for number, src in enumerate(side):
            group = number // 2
            dst = buf.at[pl.ds(number % 2 * half, half), (x + (0, xs - 1, 1, 2)[group]) & (xs - 1), at]
            count = sum(map(len, groups))
            groups[group].append(pltpu.make_async_copy(src, dst, sem.at[count]))
    return groups


def cycle_kernel(screen, rows, count, place, t_hbm, *refs):
    pieces, (out_hbm, mask, t_ref, z_ref, o_ref, t_sem, z_sem, o_sem) = refs[:16], refs[16:]
    keep, tile = screen.shape[1], z_ref.shape[-1]
    _, window, height, width = t_ref.shape
    tiles_here, tiles_wide = height // tile, width // tile
    tile_count = screen.shape[0] // window
    vir, xs = z_ref.shape[:2]
    first = place[1] * tiles_here
    moves = [pltpu.make_async_copy(t_hbm, t_ref, t_sem)]
    groups = tile_copies(place, pieces, z_ref, z_sem)
    for copy in moves + sum(groups, []):
        copy.start()
    for a in range(tiles_here):

        @pl.loop(0, mask.shape[1])
        def _(q):
            mask[a, q] = 0

        @pl.loop(0, count[first + a])
        def _(e):
            mask[a, rows[first + a, e]] = 1

    for copy in moves:
        copy.wait()

    pairs = o_ref.shape[1]

    def one(v, x):
        q = v * xs + x
        left = []
        for m in range(keep):
            u = screen[q, m]
            c = u % tile_count
            lane = pl.multiple_of((c % tiles_wide) * tile, tile)
            left.append(t_ref[c // tiles_wide, u // tile_count, :, pl.ds(lane, tile)])
        right = z_ref[v, x].reshape(keep * tile, tile)
        part = jnp.dot(jnp.concatenate(left, axis=1), right, preferred_element_type=F32)
        for a in range(tiles_here):
            here = slice(a * tile, (a + 1) * tile)
            used = jnp.full((tile, tile), mask[a, q], jnp.int32) > 0
            o_ref[x, v % pairs, v // pairs, here] = jnp.where(used, part[here], 0.0).astype(BF16)

    unroll = 16
    leaves = []
    for group, shift in zip(groups, (0, xs - 1, 1, 2), strict=True):
        for copy in group:
            copy.wait()
        x = (place[0] // 2 + shift) & (xs - 1)

        @pl.loop(0, vir // unroll)
        def _(outer):
            for inner in range(unroll):
                one(outer * unroll + inner, x)

        lanes = pl.ds(pl.multiple_of((x % tiles_wide) * tile, tile), tile)
        there = out_hbm.at[:, x // tiles_wide, :, :, lanes]
        leaves.append(pltpu.make_async_copy(o_ref.at[x], there, o_sem.at[len(leaves)]))
        leaves[-1].start()
    for copy in leaves:
        copy.wait()


def ladder_kernel(screen, slots, place, t_hbm, near_hbm, *refs):
    pieces, (out_hbm, t_ref, near_ref, w_ref, out_ref, t_sem, near_sem, w_sem, o_sem) = (
        refs[:16],
        refs[16:],
    )
    keep = screen.shape[1]
    window, blocks, _, _ = t_ref.shape
    vir, xs, cores, share = w_ref.shape[:4]
    zs = vir // xs
    per_dev = xs * cores * share
    chunks = o_sem.shape[0]
    size = blocks // chunks
    copies = sum(tile_copies(place, pieces, w_ref, w_sem), [])
    copies.append(pltpu.make_async_copy(t_hbm, t_ref, t_sem))

    def arrive(chunk):
        where = pl.ds(chunk * size, size)
        return pltpu.make_async_copy(
            near_hbm.at[:, where], near_ref.at[:, where], near_sem.at[chunk]
        )

    for copy in copies + [arrive(chunk) for chunk in range(chunks)]:
        copy.start()
    y, z = place[1] // zs, place[1] % zs
    for copy in copies:
        copy.wait()

    def one(block):
        tiles = []
        for k in range(keep):
            slot = slots[block * keep + k]
            v, within = slot // per_dev, slot % per_dev
            behind = ((y - v // zs) & (zs - 1)) * zs + ((z - v % zs) & (zs - 1))
            tiles.append(
                w_ref[behind, within // (cores * share), (within // share) % cores, within % share]
            )
        left = jnp.concatenate(tiles, axis=1)
        for j in range(window):
            right = jnp.concatenate([t_ref[j, screen[block, k]] for k in range(keep)], axis=0)
            out_ref[j, block] = near_ref[j, block].astype(F32) + jnp.dot(
                left, right, preferred_element_type=F32
            )

    unroll = 4

    def leave(chunk):
        where = pl.ds(chunk * size, size)
        return pltpu.make_async_copy(out_ref.at[:, where], out_hbm.at[:, where], o_sem.at[chunk])

    for chunk in range(chunks):
        arrive(chunk).wait()

        @pl.loop(0, size // unroll)
        def _(outer):
            for inner in range(unroll):
                one(chunk * size + outer * unroll + inner)

        leave(chunk).start()
    for chunk in range(chunks):
        leave(chunk).wait()


def final_kernel(slab, pair, place, occ_ref, base_ref, cycle_ref, va_ref, vb_ref, out_ref):
    group, window, rows, cols = cycle_ref.shape
    for g in range(group):
        here = slice(g * rows, (g + 1) * rows)
        energy_a = jnp.broadcast_to(va_ref[:, here], (128, rows)).T
        pairs = jnp.concatenate([energy_a] * (cols // 128), axis=1) + vb_ref[...]
        for j in range(window):
            below = (pairs - occ_ref[slab[place[0]]]) - occ_ref[pair[j]]
            value = base_ref[j, here] + cycle_ref[g, j].astype(F32)
            out_ref[j, here] = (value / below).astype(BF16)


def body(
    amplitudes,
    coulomb,
    ladder_tiles,
    cycle_tiles,
    ladder_screen,
    tile_slot,
    cycle_screen,
    cycle_rows,
    cycle_count,
    slab_occ,
    window_occ,
    occ_energy,
    vir_energy,
):
    occ_count, vir_count = lax.axis_size("occ"), lax.axis_size("vir")
    _, window, width_all, block_cols = amplitudes.shape
    stored, tile, _ = ladder_tiles.shape
    tile_count = width_all // tile
    rows_here = width_all // vir_count
    share = stored // occ_count
    xs, zs = occ_count // 2, 4
    occ_at, vir_at = lax.axis_index("occ"), lax.axis_index("vir")
    place = jnp.stack([occ_at, vir_at]).astype(jnp.int32)
    t = amplitudes[0]
    near = coulomb[0]

    def occ_shift(value, by):
        return lax.ppermute(value, "occ", [(i, (i + 2 * by) % occ_count) for i in range(occ_count)])

    def core_swap(value):
        return lax.ppermute(value, "occ", [(i, i ^ 1) for i in range(occ_count)])

    def vir_shift(value, dy, dz):
        ys = vir_count // zs
        return lax.ppermute(
            value,
            "vir",
            [(y * zs + z, (y + dy) % ys * zs + (z + dz) % zs) for y in range(ys) for z in range(zs)],
        )

    def ring(value, shift, size):
        return jnp.stack([value] + [shift(value, d) for d in range(1, size)])

    def spread(piece):
        half = vir_count // 2
        low, high = piece[:half], piece[half:]
        behind_low, ahead_high = occ_shift(low, 1), occ_shift(high, -1)
        behind_high, ahead_low = occ_shift(high, 1), occ_shift(low, -1)
        far_low, far_high = occ_shift(behind_low, 1), occ_shift(ahead_high, -1)
        mine = (low, high, behind_low, behind_high, ahead_low, ahead_high, far_low, far_high)
        return mine + tuple(core_swap(p) for p in mine)

    def my_share(tiles):
        return lax.dynamic_slice_in_dim(tiles, occ_at * share, share, 0)

    sent = jnp.broadcast_to(my_share(cycle_tiles)[None], (vir_count, share, tile, tile))
    cycle_piece = lax.all_to_all(sent, "vir", 0, 0, tiled=True)
    flat = t.reshape(window, vir_count, rows_here, block_cols).transpose(1, 0, 2, 3)
    ladder_share = my_share(ladder_tiles)
    line = ring(ladder_share, lambda value, by: vir_shift(value, 0, by), zs)
    flat, cycle_piece = lax.optimization_barrier((flat, cycle_piece))
    plane = ring(line, lambda value, by: vir_shift(value, by, 0), vir_count // zs)
    moved = lax.all_to_all(flat, "vir", 0, 0, tiled=True)
    cycle_parts = spread(cycle_piece)

    tile_buf = pltpu.VMEM((vir_count, xs, 2, share, tile, tile), BF16)
    dma = pltpu.SemaphoreType.DMA
    size = window * width_all * block_cols
    tile_bytes = 2 * stored * vir_count * tile * tile
    whole = (vir_count, window, rows_here, block_cols)
    paired = (vir_count // 2, 2, window, rows_here, block_cols)
    part = pl.pallas_call(
        cycle_kernel,
        out_shape=pltpu.HBM(paired, BF16),
        grid_spec=pltpu.PrefetchScalarGridSpec(
            num_scalar_prefetch=4,
            grid=(1,),
            in_specs=[ANY] * 17,
            out_specs=ANY,
            scratch_shapes=[
                pltpu.SMEM((rows_here // tile, window * tile_count), jnp.int32),
                pltpu.VMEM(whole, BF16),
                tile_buf,
                pltpu.VMEM((xs, vir_count // 2, window, rows_here, tile), BF16),
                dma(()),
                dma((16,)),
                dma((4,)),
            ],
        ),
        compiler_params=room(60),
        cost_estimate=cost(8 * size * tile, 4 * size + tile_bytes),
    )(cycle_screen, cycle_rows, cycle_count, place, moved, *cycle_parts)
    cycle = lax.all_to_all(part.reshape(whole), "vir", 0, 0, tiled=True)

    ladder_parts = spread(plane.reshape(vir_count, share, tile, tile))
    blocked = (window, tile_count, tile, block_cols)
    base = pl.pallas_call(
        ladder_kernel,
        out_shape=pltpu.HBM(blocked, F32),
        grid_spec=pltpu.PrefetchScalarGridSpec(
            num_scalar_prefetch=3,
            grid=(1,),
            in_specs=[ANY] * 18,
            out_specs=ANY,
            scratch_shapes=[
                pltpu.VMEM(blocked, BF16),
                pltpu.VMEM(blocked, BF16),
                tile_buf,
                pltpu.VMEM(blocked, F32),
                dma(()),
                dma((4,)),
                dma((16,)),
                dma((4,)),
            ],
        ),
        compiler_params=room(60),
        cost_estimate=cost(16 * size * tile, 8 * size + tile_bytes),
    )(ladder_screen, tile_slot, place, t.reshape(blocked), near.reshape(blocked), *ladder_parts)

    energies = vir_energy.reshape(1, width_all)
    group = 8
    out = pl.pallas_call(
        final_kernel,
        out_shape=jax.ShapeDtypeStruct(t.shape, BF16),
        grid_spec=pltpu.PrefetchScalarGridSpec(
            num_scalar_prefetch=3,
            grid=(vir_count // group,),
            in_specs=[
                SCALARS,
                pl.BlockSpec((window, group * rows_here, block_cols), lambda g, *_: (0, g, 0)),
                pl.BlockSpec((group, window, rows_here, block_cols), lambda g, *_: (g, 0, 0, 0)),
                pl.BlockSpec((1, group * rows_here), lambda g, *_: (0, g)),
                pl.BlockSpec((1, block_cols), lambda g, slab, pair, place: (0, place[1])),
            ],
            out_specs=pl.BlockSpec(
                (window, group * rows_here, block_cols), lambda g, *_: (0, g, 0)
            ),
        ),
        compiler_params=room(60),
        cost_estimate=cost(8 * size, 8 * size),
    )(
        slab_occ,
        window_occ,
        place,
        occ_energy,
        base.reshape(t.shape),
        cycle,
        energies,
        energies,
    )
    return out[None]


def solution(mesh):
    wide = P("occ", None, None, "vir")
    tiles = P("vir", None, None)
    return jax.shard_map(
        body,
        mesh=mesh,
        in_specs=(wide, wide, tiles, tiles) + (P(),) * 9,
        out_specs=wide,
        check_vma=False,
    )
```
